32 devices in a mesh: groups: 2 (over x), row: 8 (over z, y), col: 2 (over core).
Axes of the slice: x: 2, y: 2, z: 4, core: 2. Of those that a mesh axis runs over, the one named last changes fastest.
Arguments:
- tokens_in: bfloat16 [16, 256, 768], P('groups', 'row'), parts along dimension 0, may hold values from -6 to 6
- cond_single: bfloat16 [512, 768], P(('groups', 'row')), parts along dimension 0, may hold values from -6 to 6
- token_mask: int32 [512], P(('groups', 'row')), parts along dimension 0, may hold values 0 or 1
- pair_cond: bfloat16 [512, 256, 128], P(('groups', 'row'), 'col'), parts along dimension 0, may hold values from -1000 to 1000
- w_pair: bfloat16 [128, 16], replicated, may hold values from -0.5 to 0.5
- w_scale: bfloat16 [768, 768], replicated, may hold values from -0.21875 to 0.21875
- w_shift: bfloat16 [768, 768], replicated, may hold values from -0.21875 to 0.21875
- w_outgate: bfloat16 [768, 768], replicated, may hold values from -0.21875 to 0.21875
- w_query: bfloat16 [768, 768], P(None, 'col'), may hold values from -0.21875 to 0.21875
- w_key: bfloat16 [768, 768], P(None, 'col'), may hold values from -0.21875 to 0.21875
- w_value: bfloat16 [768, 768], P(None, 'col'), may hold values from -0.21875 to 0.21875
- w_gate: bfloat16 [768, 768], P(None, 'col'), may hold values from -0.21875 to 0.21875
- w_out: bfloat16 [768, 768], P('col'), may hold values from -0.21875 to 0.21875
- atom_cond: bfloat16 [4096, 128], P(('groups', 'row', 'col')), parts along dimension 0, may hold values from -6 to 6
- atom_token: int32 [4096], P(('groups', 'row', 'col')), parts along dimension 0, may hold values from 0 to 255, as said below
- window_start: int32 [128], P(('groups', 'row', 'col')), parts along dimension 0, may hold values from 0 to 1920, as said below
- atom_mask: int32 [4096], P(('groups', 'row', 'col')), parts along dimension 0, may hold values 0 or 1
- atom_pair: bfloat16 [128, 16, 32, 128], P(('groups', 'row', 'col')), parts along dimension 0, may hold values from -1000 to 1000
- w_token_atom: bfloat16 [768, 128], replicated, may hold values from -0.21875 to 0.21875
- w_ascale: bfloat16 [128, 128], replicated, may hold values from -0.5 to 0.5
- w_ashift: bfloat16 [128, 128], replicated, may hold values from -0.5 to 0.5
- w_aquery: bfloat16 [128, 128], replicated, may hold values from -0.5 to 0.5
- w_akey: bfloat16 [128, 128], replicated, may hold values from -0.5 to 0.5
- w_avalue: bfloat16 [128, 128], replicated, may hold values from -0.5 to 0.5
- w_agate: bfloat16 [128, 128], replicated, may hold values from -0.5 to 0.5
- w_aout: bfloat16 [128, 128], replicated, may hold values from -0.5 to 0.5
- w_apair: bfloat16 [16, 4], replicated, may hold values from -1.5 to 1.5
- w_update: bfloat16 [3, 128], replicated, may hold values from -0.5 to 0.5
Outputs:
- tokens_out: bfloat16 [16, 256, 768], P('groups', 'row'), parts along dimension 0
- atom_update: float32 [16, 3, 2048], P('groups', None, ('row', 'col')), parts along dimension 0
The draws below stay inside these ranges and needn't reach their ends.
There are 2 independent parts, one for each index of `groups`. The reference program is written for one: setup_inputs(seed, part) draws one part's arguments, and reference() takes and returns one part's arrays. A program takes and returns all parts, laid end to end along the dimension named above; an argument that names none is the same for every part. Nothing has to cross between parts.
Inputs may be any that keep to these rules, and one draw needn't show every extreme that they name: atom_token[l] differs from l // 8 by at most 16. window_start[k] differs from k * 32 + 32 // 2 - 128 // 2 by at most 16, unless it is clipped to the range.
All inputs are finite; a program needn't handle non-finite values. No bound on the sum of `token_mask` or of `atom_mask` on one device may be relied on, other than what follows from the above.
Results may differ from the reference program's by a relative error of at most 0.0075.
Values may be sent and summed in bfloat16 or wider, within the bound.
No kernel may reach another device: no remote copies, remote signals or barrier semaphores. Data moves between devices by JAX's collectives and lax.ppermute only.
A program may use at most 128 MiB of HBM per device.

```python
import jax
import jax.numpy as jnp
from jax import lax

D = 768
HEADS = 16
HEAD = 48
CZ = 128
DA = 128
AHEADS = 4
AHEAD = 32
CP = 16
WQ = 32
WK = 128
PER_TOKEN = 8
TOK_ROW = 32
SAMPLES = 8
TOKENS = 256
ATOMS = 2048
WINDOWS = 64


def draw_pair_cond(key, part):
    key_one = jax.random.fold_in(key, 0)
    normals = jax.random.normal(key_one, (TOKENS, TOKENS, CZ), jnp.float32)
    return jnp.clip(normals, -1000.0, 1000.0).astype(jnp.bfloat16)


def draw_atom_pair(key, part):
    key_one = jax.random.fold_in(key, 0)
    normals = jax.random.normal(key_one, (WINDOWS, CP, WQ, WK), jnp.float32)
    return jnp.clip(normals, -1000.0, 1000.0).astype(jnp.bfloat16)


def draw_atom_token(key, part):
    reach = TOK_ROW // 2
    position = jnp.arange(ATOMS, dtype=jnp.int32) // PER_TOKEN
    jitter = jax.random.randint(key, (ATOMS,), -reach, reach + 1, dtype=jnp.int32)
    token_ids = jnp.clip(position + jitter, 0, TOKENS - 1)
    middle = ATOMS // 2
    token_ids = token_ids.at[middle].set(middle // PER_TOKEN + reach)
    token_ids = token_ids.at[middle + 1].set((middle + 1) // PER_TOKEN - reach)
    token_ids = token_ids.at[0].set(0).at[ATOMS - 1].set(TOKENS - 1)
    return token_ids.astype(jnp.int32)


def draw_window_start(key, part):
    window_index = jnp.arange(WINDOWS, dtype=jnp.int32)
    jitter = jax.random.randint(key, (WINDOWS,), -(WQ // 2), WQ // 2 + 1, dtype=jnp.int32)
    return jnp.clip(window_index * WQ + WQ // 2 - WK // 2 + jitter, 0, ATOMS - WK).astype(jnp.int32)


def with_ends(drawn, stream_key, least, largest):
    longest = drawn.shape.index(max(drawn.shape))
    spots = []
    for shift in (0, 1):
        where = [jax.random.randint(jax.random.fold_in(stream_key, axis), (), 0, length) for axis, length in enumerate(drawn.shape)]
        where[longest] = (where[longest] + shift) % drawn.shape[longest]
        spots.append(tuple(where))
    return drawn.at[spots[0]].set(least).at[spots[1]].set(largest)


def level_of(stream_key, extent, cuts, smallest, top_value):
    factor_of, own = 1.0, jax.random.fold_in(stream_key, 6)
    for dim, shards_of in cuts:
        draws = jnp.exp(jax.random.uniform(jax.random.fold_in(own, dim), (shards_of,), jnp.float32, smallest / len(cuts), top_value / len(cuts)))
        factor_of = factor_of * jnp.repeat(draws, extent[dim] // shards_of).reshape([-1 if axis == dim else 1 for axis in range(len(extent))])
    return factor_of


def noise(own_key, dims, deviation, most, pieces=(), kind=jnp.bfloat16):
    drawn = deviation * jax.random.normal(own_key, dims, jnp.float32)
    if pieces:
        drawn = drawn * level_of(own_key, dims, pieces, -0.22, 0.18)
    return jnp.clip(drawn, -most, most).astype(kind)


def setup_inputs(seed: int = 0, part: int = 0) -> dict:
    keys = jax.random.split(jax.random.key(seed), 29)
    part_keys = jax.random.split(jax.random.fold_in(keys[28], part), 29)
    return {
        "tokens_in": noise(part_keys[0], (SAMPLES, TOKENS, D), 1.0, 6.0, ((1, 8),)),
        "cond_single": noise(part_keys[1], (TOKENS, D), 1.0, 6.0, ((0, 8),)),
        "token_mask": with_ends((jax.random.randint(part_keys[2], (TOKENS,), 0, 8) < 7).astype(jnp.int32), jax.random.fold_in(part_keys[2], 1), 0, 1),
        "pair_cond": draw_pair_cond(jax.random.fold_in(jax.random.fold_in(keys[28], part), 71), part),
        "w_pair": noise(keys[4], (CZ, HEADS), CZ ** -0.5, 0.5),
        "w_scale": noise(keys[5], (D, D), D ** -0.5, 0.21875),
        "w_shift": noise(keys[6], (D, D), D ** -0.5, 0.21875),
        "w_outgate": noise(keys[7], (D, D), D ** -0.5, 0.21875),
        "w_query": noise(keys[8], (D, D), D ** -0.5, 0.21875, ((1, 2),)),
        "w_key": noise(keys[9], (D, D), D ** -0.5, 0.21875, ((1, 2),)),
        "w_value": noise(keys[10], (D, D), D ** -0.5, 0.21875, ((1, 2),)),
        "w_gate": noise(keys[11], (D, D), D ** -0.5, 0.21875, ((1, 2),)),
        "w_out": noise(keys[12], (D, D), D ** -0.5, 0.21875, ((0, 2),)),
        "atom_cond": noise(part_keys[13], (ATOMS, DA), 1.0, 6.0, ((0, 16),)),
        "atom_token": draw_atom_token(jax.random.fold_in(jax.random.fold_in(keys[28], part), 71), part),
        "window_start": draw_window_start(jax.random.fold_in(jax.random.fold_in(keys[28], part), 71), part),
        "atom_mask": with_ends((jax.random.randint(part_keys[16], (ATOMS,), 0, 8) < 7).astype(jnp.int32), jax.random.fold_in(part_keys[16], 1), 0, 1),
        "atom_pair": draw_atom_pair(jax.random.fold_in(jax.random.fold_in(keys[28], part), 71), part),
        "w_token_atom": noise(keys[18], (D, DA), D ** -0.5, 0.21875),
        "w_ascale": noise(keys[19], (DA, DA), DA ** -0.5, 0.5),
        "w_ashift": noise(keys[20], (DA, DA), DA ** -0.5, 0.5),
        "w_aquery": noise(keys[21], (DA, DA), DA ** -0.5, 0.5),
        "w_akey": noise(keys[22], (DA, DA), DA ** -0.5, 0.5),
        "w_avalue": noise(keys[23], (DA, DA), DA ** -0.5, 0.5),
        "w_agate": noise(keys[24], (DA, DA), DA ** -0.5, 0.5),
        "w_aout": noise(keys[25], (DA, DA), DA ** -0.5, 0.5),
        "w_apair": noise(keys[26], (CP, AHEADS), CP ** -0.5, 1.5),
        "w_update": noise(keys[27], (3, DA), DA ** -0.5, 0.5),
    }


def layer_norm(inputs):
    inputs = inputs.astype(jnp.float32)
    centred = inputs - lax.optimization_barrier(jnp.mean(inputs, axis=-1, keepdims=True))
    variance = lax.optimization_barrier(jnp.mean(centred * centred, axis=-1, keepdims=True))
    return centred * lax.rsqrt(variance + 1e-05)

def rounded(inputs):
    return lax.optimization_barrier(inputs.astype(jnp.bfloat16)).astype(jnp.float32)

def reference(tokens_in, cond_single, token_mask, pair_cond, w_pair, w_scale, w_shift, w_outgate, w_query, w_key, w_value, w_gate, w_out, atom_cond, atom_token, window_start, atom_mask, atom_pair, w_token_atom, w_ascale, w_ashift, w_aquery, w_akey, w_avalue, w_agate, w_aout, w_apair, w_update):
    highest = lax.Precision.HIGHEST
    cond_norm = layer_norm(cond_single).astype(jnp.bfloat16)
    ada_scale = jax.nn.sigmoid(jnp.dot(cond_norm, w_scale, preferred_element_type=jnp.float32))
    ada_shift = jnp.dot(cond_norm, w_shift, preferred_element_type=jnp.float32)
    out_gate = jax.nn.sigmoid(jnp.dot(cond_norm, w_outgate, preferred_element_type=jnp.float32))
    pair_float = w_pair.astype(jnp.float32)
    pair_bias = lax.map(lambda pair_rows: jnp.dot(pair_rows.astype(jnp.float32), pair_float, precision=highest).T, pair_cond)
    mask_shift = (token_mask.astype(jnp.float32) - 1.0) * 10000.0
    inv_root = HEAD ** (-0.5)

    def token_sample(sample_rows):
        mixed_rows = (ada_scale * layer_norm(sample_rows) + ada_shift).astype(jnp.bfloat16)
        queries = (jnp.dot(mixed_rows, w_query, preferred_element_type=jnp.float32) * inv_root).astype(jnp.bfloat16).reshape(TOKENS, HEADS, HEAD)
        key_rows = jnp.dot(mixed_rows, w_key, preferred_element_type=jnp.float32).astype(jnp.bfloat16).reshape(TOKENS, HEADS, HEAD)
        value_rows = jnp.dot(mixed_rows, w_value, preferred_element_type=jnp.float32).astype(jnp.bfloat16).reshape(TOKENS, HEADS, HEAD)
        head_gate = jax.nn.sigmoid(jnp.dot(mixed_rows, w_gate, preferred_element_type=jnp.float32))
        scores = jnp.einsum('qhd,khd->qhk', queries.astype(jnp.float32), key_rows.astype(jnp.float32), precision=highest) + pair_bias + mask_shift
        row_max = lax.optimization_barrier(jnp.max(scores, axis=-1, keepdims=True))
        weights = jnp.exp(scores - row_max)
        totals = lax.optimization_barrier(jnp.sum(weights, axis=-1, keepdims=True))
        attended = jnp.einsum('qhk,khd->qhd', rounded(weights), value_rows.astype(jnp.float32), precision=highest) / totals
        gated = (head_gate * attended.reshape(TOKENS, D)).astype(jnp.bfloat16)
        update = jnp.dot(gated, w_out, preferred_element_type=jnp.float32)
        return (sample_rows.astype(jnp.float32) + out_gate * update).astype(jnp.bfloat16)
    tokens_out = lax.map(token_sample, tokens_in)

    def project_rows(sample_rows):
        token_norm = layer_norm(sample_rows).astype(jnp.bfloat16)
        return jnp.dot(token_norm, w_token_atom, preferred_element_type=jnp.float32).astype(jnp.bfloat16)
    token_proj = lax.map(project_rows, tokens_out)
    cond_anorm = layer_norm(atom_cond).astype(jnp.bfloat16)
    atom_scale = jax.nn.sigmoid(jnp.dot(cond_anorm, w_ascale, preferred_element_type=jnp.float32))
    atom_shift = jnp.dot(cond_anorm, w_ashift, preferred_element_type=jnp.float32)
    atom_bias = jnp.einsum('wcqk,ch->whqk', atom_pair.astype(jnp.float32), w_apair.astype(jnp.float32), precision=highest)
    key_index = window_start[:, None].astype(jnp.int32) + jnp.arange(WK, dtype=jnp.int32)[None, :]
    atom_root = AHEAD ** (-0.5)
    live = atom_mask.astype(jnp.float32)

    def atom_sample(projected):
        atom_state = atom_cond.astype(jnp.float32) + projected[atom_token].astype(jnp.float32)
        atom_mixed = (atom_scale * layer_norm(atom_state) + atom_shift).astype(jnp.bfloat16)
        queries = (jnp.dot(atom_mixed, w_aquery, preferred_element_type=jnp.float32) * atom_root).astype(jnp.bfloat16).reshape(WINDOWS, WQ, AHEADS, AHEAD)
        key_rows = jnp.dot(atom_mixed, w_akey, preferred_element_type=jnp.float32).astype(jnp.bfloat16).reshape(ATOMS, AHEADS, AHEAD)[key_index]
        value_rows = jnp.dot(atom_mixed, w_avalue, preferred_element_type=jnp.float32).astype(jnp.bfloat16).reshape(ATOMS, AHEADS, AHEAD)[key_index]
        atom_gate = jax.nn.sigmoid(jnp.dot(atom_mixed, w_agate, preferred_element_type=jnp.float32))
        scores = jnp.einsum('wqhd,wkhd->whqk', queries.astype(jnp.float32), key_rows.astype(jnp.float32), precision=highest) + atom_bias
        row_max = lax.optimization_barrier(jnp.max(scores, axis=-1, keepdims=True))
        weights = jnp.exp(scores - row_max)
        totals = lax.optimization_barrier(jnp.sum(weights, axis=-1, keepdims=True))
        attended = jnp.einsum('whqk,wkhd->wqhd', rounded(weights), value_rows.astype(jnp.float32), precision=highest) / jnp.transpose(totals, (0, 2, 1, 3))
        gated = (atom_gate * attended.reshape(ATOMS, DA)).astype(jnp.bfloat16)
        atom_final = atom_state + jnp.dot(gated, w_aout, preferred_element_type=jnp.float32)
        final_norm = layer_norm(atom_final).astype(jnp.bfloat16)
        return jnp.dot(w_update, final_norm.T, preferred_element_type=jnp.float32) * live[None, :]
    atom_update = lax.map(atom_sample, token_proj)
    return (tokens_out, atom_update)
```

```python
import functools

import jax
import jax.numpy as jnp
from jax import lax
from jax.experimental import pallas as pl
from jax.experimental.pallas import tpu as pltpu
from jax.sharding import PartitionSpec as P

HEAD = 48
AHEADS = 4
AHEAD = 32
WQ = 32
WK = 128
HALO = WK // 2
SPAN = 2 * WK
PER_TOKEN = 8
F32 = jnp.float32
BF16 = jnp.bfloat16
NT = (((1,), (1,)), ((), ()))


def layer_norm(inputs):
    inputs = inputs.astype(F32)
    centred = inputs - jnp.mean(inputs, axis=-1, keepdims=True)
    variance = jnp.mean(centred * centred, axis=-1, keepdims=True)
    return centred * lax.rsqrt(variance + 1e-05)


def dot(a, b):
    return jnp.dot(a, b, preferred_element_type=F32)


def whole(array):
    zeros = (0,) * array.ndim
    return pl.BlockSpec(array.shape, lambda *_: zeros)


def of(shape, dtype):
    return jax.ShapeDtypeStruct(shape, dtype)


def mix_kernel(col_ref, tok_ref, cond_ref, scale_ref, shift_ref, valid_ref, out_ref):
    samples, rows, _ = tok_ref.shape
    cond_norm = layer_norm(cond_ref[...]).astype(BF16)
    scale = jax.nn.sigmoid(dot(cond_norm, scale_ref[...]))
    shift = dot(cond_norm, shift_ref[...])
    for s in range(samples):
        mixed = scale * layer_norm(tok_ref[s]) + shift
        out_ref[s * rows : (s + 1) * rows, :] = mixed.astype(BF16)
    out_ref[samples * rows :, :] = valid_ref[...]


def mix(col, tokens_in, cond, w_scale, w_shift, valid, local_samples):
    _, rows, width = tokens_in.shape
    total = local_samples * rows + valid.shape[0]
    return pl.pallas_call(
        mix_kernel,
        grid_spec=pltpu.PrefetchScalarGridSpec(
            num_scalar_prefetch=1,
            grid=(1,),
            in_specs=[
                pl.BlockSpec((local_samples, rows, width), lambda i, c: (c[0], 0, 0)),
                whole(cond),
                whole(w_scale),
                whole(w_shift),
                whole(valid),
            ],
            out_specs=pl.BlockSpec((total, width), lambda i, c: (0, 0)),
        ),
        out_shape=of((total, width), BF16),
        name="mix",
    )(col, tokens_in, cond, w_scale, w_shift, valid)


def kv_kernel(count, aliased, place_ref, *refs):
    blocks, refs = refs[:count], refs[count:]
    weights, refs = refs[:4], refs[4:]
    key_ref, value_ref = refs[2:] if aliased else refs
    samples, rows, _ = key_ref.shape
    block = blocks[0][...]
    if count == 2:
        first = pl.program_id(0) == 0
        block = jnp.where(first, block, blocks[1][...])
    half = weights[0].shape[1]
    for index, weight in enumerate(weights):
        out = dot(block, weight[...]).astype(BF16).reshape(samples, rows, half)
        target = key_ref if index < 2 else value_ref
        start = (index % 2) * half
        target[:, :, start : start + half] = out


def project_kv(place, base, blocks, weights, held, samples, rows, keys):
    count = len(blocks)
    width = blocks[0].shape[1]
    aliased = held is not None
    held = held or ()
    out_spec = pl.BlockSpec((samples, rows, width), lambda i, p: (0, p[base + i], 0))
    return pl.pallas_call(
        functools.partial(kv_kernel, count, aliased),
        grid_spec=pltpu.PrefetchScalarGridSpec(
            num_scalar_prefetch=1,
            grid=(count,),
            in_specs=[pl.BlockSpec((samples * rows, width), lambda i, p: (0, 0))] * count
            + [whole(w) for w in weights]
            + [pl.BlockSpec(memory_space=pl.ANY)] * len(held),
            out_specs=[out_spec, out_spec],
        ),
        out_shape=[of((samples, keys, width), BF16)] * 2,
        input_output_aliases={1 + count + 4 + i: i for i in range(len(held))},
        name="project_kv",
    )(place, *blocks, *weights, *held)


def query_kernel(root, block_ref, ql_ref, qr_ref, gl_ref, gr_ref, cond_ref, og_ref, q_ref, g_ref, o_ref):
    block = block_ref[...]
    half = ql_ref.shape[1]
    q_ref[:, :half] = (dot(block, ql_ref[...]) * root).astype(BF16)
    q_ref[:, half:] = (dot(block, qr_ref[...]) * root).astype(BF16)
    g_ref[:, :half] = jax.nn.sigmoid(dot(block, gl_ref[...]))
    g_ref[:, half:] = jax.nn.sigmoid(dot(block, gr_ref[...]))
    cond_norm = layer_norm(cond_ref[...]).astype(BF16)
    o_ref[...] = jax.nn.sigmoid(dot(cond_norm, og_ref[...]))


def project_q(block, weights, cond, w_outgate, count):
    width = block.shape[1]
    rows = cond.shape[0]
    return pl.pallas_call(
        functools.partial(query_kernel, HEAD ** (-0.5)),
        grid=(1,),
        in_specs=[pl.BlockSpec((count, width), lambda i: (0, 0))]
        + [whole(w) for w in weights]
        + [whole(cond), whole(w_outgate)],
        out_specs=[pl.BlockSpec((count, width), lambda i: (0, 0))] * 2
        + [pl.BlockSpec((rows, width), lambda i: (0, 0))],
        out_shape=[of((count, width), BF16), of((count, width), F32), of((rows, width), F32)],
        name="project_q",
    )(block, *weights, cond, w_outgate)


def bias_kernel(pair_ref, w_ref, out_ref):
    rows, keys, channels = pair_ref.shape
    for i in range(rows):
        out_ref[:, i, :] = lax.dot_general(
            w_ref[...], pair_ref[i], NT, preferred_element_type=F32
        )


def pair_bias_of(pair_cond, w_pair):
    rows, keys, _ = pair_cond.shape
    heads = w_pair.shape[1]
    return pl.pallas_call(
        bias_kernel, out_shape=of((heads, rows, keys), F32), name="pair_bias"
    )(pair_cond, w_pair.T)


def head_lanes(shape, start, head, size):
    lane = lax.broadcasted_iota(jnp.int32, shape, 1) + start
    return (lane >= head * size) & (lane < (head + 1) * size)


def attend_kernel(
    blocks, valid_width, col_ref, q_ref, k_ref, v_ref, bl_ref, br_ref, g_ref, o_ref, tok_ref, wol_ref,
    wor_ref, wta_ref, *refs,
):
    valid_refs, (out_ref, proj_ref, gated_ref) = refs[:blocks], refs[blocks:]
    s = pl.program_id(0)
    col = col_ref[0]
    rows, width = q_ref.shape
    heads = bl_ref.shape[0]
    half = heads // 2
    query = q_ref[...].astype(F32)
    spread = jnp.concatenate(
        [
            jnp.where(head_lanes((rows, width), 0, h, HEAD), query, 0.0).astype(BF16)
            for h in range(heads)
        ],
        axis=0,
    )
    keys = k_ref[0]
    scores = lax.dot_general(spread, keys, NT, preferred_element_type=F32)
    valid = valid_refs[0][...].astype(F32)
    for ref in valid_refs[1:]:
        valid = valid + ref[...].astype(F32)
    count = keys.shape[0]
    shift = jnp.concatenate(
        [valid[i : i + 1, :valid_width] for i in range(count // valid_width)], axis=1
    )
    shift = (shift - 1.0) * 10000.0
    near = pl.multiple_of(col * half, half)
    far = pl.multiple_of((1 - col) * half, half)
    bias = jnp.concatenate(
        [
            jnp.concatenate([ref[pl.ds(near, half)], ref[pl.ds(far, half)]], axis=0).reshape(
                heads * rows, ref.shape[2]
            )
            for ref in (bl_ref, br_ref)
        ],
        axis=1,
    )
    scores = scores + bias + shift
    weights = jnp.exp(scores - jnp.max(scores, axis=-1, keepdims=True))
    totals = jnp.sum(weights, axis=-1, keepdims=True)
    weights = weights.astype(BF16)
    start = pl.multiple_of(s * rows, rows)
    for lane in range(0, width, 128):
        low, high = lane // HEAD, (lane + 127) // HEAD + 1
        part = dot(weights[low * rows : high * rows], v_ref[0, :, lane : lane + 128])
        attended = jnp.zeros((rows, 128), F32)
        for h in range(low, high):
            mine = part[(h - low) * rows : (h - low + 1) * rows] / totals[h * rows : (h + 1) * rows]
            attended = attended + jnp.where(head_lanes((rows, 128), lane, h, HEAD), mine, 0.0)
        gate = g_ref[pl.ds(start, rows), lane : lane + 128]
        gated_ref[pl.ds(start, rows), lane : lane + 128] = (gate * attended).astype(BF16)

    @pl.when(s == pl.num_programs(0) - 1)
    def _():
        gated = gated_ref[...]
        middle = wol_ref.shape[0]
        update = dot(gated[:, :middle], wol_ref[...]) + dot(gated[:, middle:], wor_ref[...])
        samples = tok_ref.shape[0]
        for n in range(samples):
            tokens = tok_ref[n].astype(F32) + o_ref[...] * update[n * rows : (n + 1) * rows]
            tokens = tokens.astype(BF16)
            out_ref[n] = tokens
            proj_ref[n] = dot(layer_norm(tokens).astype(BF16), wta_ref[...]).astype(BF16)


def attend(col, query, keys, values, near, far, gate, out_gate, tokens_in, outs, w_token_atom, blocks, valid_width):
    samples, count, width = keys.shape
    rows = query.shape[0] // samples
    atoms = w_token_atom.shape[1]
    per_sample = pl.BlockSpec((1, count, width), lambda s, c: (s, 0, 0))
    valid_row = samples * rows // 8
    return pl.pallas_call(
        functools.partial(attend_kernel, len(blocks), valid_width),
        grid_spec=pltpu.PrefetchScalarGridSpec(
            num_scalar_prefetch=1,
            grid=(samples,),
            in_specs=[
                pl.BlockSpec((rows, width), lambda s, c: (s, 0)),
                per_sample,
                per_sample,
                whole(near),
                whole(far),
                whole(gate),
                whole(out_gate),
                pl.BlockSpec((samples, rows, width), lambda s, c: (c[0], 0, 0)),
                whole(outs[0]),
                whole(outs[1]),
                whole(w_token_atom),
            ]
            + [pl.BlockSpec((8, width), lambda s, c: (valid_row, 0))] * len(blocks),
            out_specs=[
                pl.BlockSpec((samples, rows, width), lambda s, c: (0, 0, 0)),
                pl.BlockSpec((samples, rows, atoms), lambda s, c: (0, 0, 0)),
            ],
            scratch_shapes=[pltpu.VMEM((samples * rows, width), BF16)],
        ),
        out_shape=[of((samples, rows, width), BF16), of((samples, rows, atoms), BF16)],
        name="attend",
    )(col, query, keys, values, near, far, gate, out_gate, tokens_in, *outs, w_token_atom, *blocks)


def atom_bias_kernel(w_ref, pair_ref, out_ref):
    windows, channels, rows, keys = pair_ref.shape
    heads = w_ref.shape[1]

    def window(k, carry):
        pair = [pair_ref[k, c].astype(F32) for c in range(channels)]
        for h in range(heads):
            total = pair[0] * w_ref[0, h]
            for c in range(1, channels):
                total = total + pair[c] * w_ref[c, h]
            out_ref[k, h * rows : (h + 1) * rows, :] = total
        return carry

    lax.fori_loop(0, windows, window, 0)


def atom_bias_of(atom_pair, w_apair):
    windows, _, rows, keys = atom_pair.shape
    heads = w_apair.shape[1]
    return pl.pallas_call(
        atom_bias_kernel,
        in_specs=[pl.BlockSpec(memory_space=pltpu.SMEM), pl.BlockSpec(memory_space=pltpu.VMEM)],
        out_shape=of((windows, heads * rows, keys), F32),
        name="atom_bias",
    )(w_apair.astype(F32), atom_pair)


def atom_cond_kernel(cond_ref, scale_ref, shift_ref, out_scale_ref, out_shift_ref):
    cond_norm = layer_norm(cond_ref[...]).astype(BF16)
    out_scale_ref[...] = jax.nn.sigmoid(dot(cond_norm, scale_ref[...]))
    out_shift_ref[...] = dot(cond_norm, shift_ref[...])


def atom_cond_of(cond, w_ascale, w_ashift):
    return pl.pallas_call(
        atom_cond_kernel, out_shape=[of(cond.shape, F32)] * 2, name="atom_cond"
    )(cond, w_ascale, w_ashift)


def atom_kernel(
    col_ref, left_ref, own_ref, right_ref, pick_ref, win_ref, cond_ref, scale_ref, shift_ref, bias_ref,
    live_ref, wq_ref, wk_ref, wv_ref, wg_ref, wo_ref, wu_ref, keep_ref, send_ref,
):
    samples = own_ref.shape[0]
    extent, width = cond_ref.shape
    windows = win_ref.shape[0]
    atoms = windows * WQ
    pick = pick_ref[...]
    cond = cond_ref[...].astype(F32)
    scale, shift = scale_ref[...], shift_ref[...]
    root = AHEAD ** (-0.5)
    mine = col_ref[0] == 0
    for s in range(samples):
        lookup = jnp.concatenate([left_ref[s], own_ref[s], right_ref[s]], axis=0)
        state = cond + dot(pick, lookup)
        mixed = (scale * layer_norm(state) + shift).astype(BF16)
        inner = mixed[HALO : HALO + atoms]
        query = dot(inner, wq_ref[...]) * root
        gate = jax.nn.sigmoid(dot(inner, wg_ref[...]))
        keys = dot(mixed, wk_ref[...]).astype(BF16)
        values = dot(mixed, wv_ref[...]).astype(BF16)
        pieces = []
        for k in range(windows):
            base = min(max(k * WQ - WQ, 0), extent - SPAN)
            window = win_ref[k]
            window_keys = dot(window, keys[base : base + SPAN]).astype(BF16)
            window_values = dot(window, values[base : base + SPAN]).astype(BF16)
            own = query[k * WQ : (k + 1) * WQ]
            spread = jnp.concatenate(
                [
                    jnp.where(head_lanes((WQ, width), 0, h, AHEAD), own, 0.0).astype(BF16)
                    for h in range(AHEADS)
                ],
                axis=0,
            )
            scores = lax.dot_general(spread, window_keys, NT, preferred_element_type=F32)
            scores = scores + bias_ref[k]
            weights = jnp.exp(scores - jnp.max(scores, axis=-1, keepdims=True))
            totals = jnp.sum(weights, axis=-1, keepdims=True)
            part = dot(weights.astype(BF16), window_values) / totals
            attended = jnp.zeros((WQ, width), F32)
            for h in range(AHEADS):
                attended = attended + jnp.where(
                    head_lanes((WQ, width), 0, h, AHEAD), part[h * WQ : (h + 1) * WQ], 0.0
                )
            pieces.append(attended)
        gated = (gate * jnp.concatenate(pieces, axis=0)).astype(BF16)
        final = state[HALO : HALO + atoms] + dot(gated, wo_ref[...])
        final = layer_norm(final).astype(BF16)
        update = lax.dot_general(wu_ref[...], final, NT, preferred_element_type=F32)
        update = update * live_ref[...]
        near, far = update[:, : atoms // 2], update[:, atoms // 2 :]
        keep_ref[s] = jnp.where(mine, near, far)
        send_ref[s] = jnp.where(mine, far, near)


def decode(col, left, own, right, pick, window, cond, scale, shift, bias, live, weights):
    samples = own.shape[0]
    atoms = window.shape[0] * WQ
    outputs = weights[-1].shape[0]
    vmem = pl.BlockSpec(memory_space=pltpu.VMEM)
    return pl.pallas_call(
        atom_kernel,
        in_specs=[pl.BlockSpec(memory_space=pltpu.SMEM)] + [vmem] * (10 + len(weights)),
        out_shape=[of((samples, outputs, atoms // 2), F32)] * 2,
        name="decode",
    )(col, left, own, right, pick, window, cond, scale, shift, bias, live, *weights)


def shards(
    tokens_in,
    cond_single,
    token_mask,
    pair_cond,
    w_pair,
    w_scale,
    w_shift,
    w_outgate,
    w_query,
    w_key,
    w_value,
    w_gate,
    w_out,
    atom_cond,
    atom_token,
    window_start,
    atom_mask,
    atom_pair,
    w_token_atom,
    w_ascale,
    w_ashift,
    w_aquery,
    w_akey,
    w_avalue,
    w_agate,
    w_aout,
    w_apair,
    w_update,
):
    samples, rows, width = tokens_in.shape
    count = lax.axis_size("row")
    local = samples // lax.axis_size("col")
    row, col = lax.axis_index("row"), lax.axis_index("col")
    col_index = col.astype(jnp.int32).reshape(1)
    keys = count * rows

    def swap(array):
        return lax.ppermute(array, "col", [(0, 1), (1, 0)])

    def in_order(array, axis):
        other = swap(array)
        return jnp.where(
            col == 0,
            jnp.concatenate([array, other], axis=axis),
            jnp.concatenate([other, array], axis=axis),
        )

    half = count // 2
    ring = list(range(0, count, 2)) + list(range(count - 1, 0, -2))
    forward = [(ring[p], ring[(p + 1) % count]) for p in range(count)]
    backward = [(b, a) for a, b in forward]
    position = jnp.where(row % 2 == 0, row // 2, half + (count - 1 - row) // 2)
    steps = [0]
    for k in range(1, half + 1):
        steps += [k, -k] if k < half else [k]
    source = (position - jnp.array(steps, jnp.int32)) % count
    source = jnp.where(source < half, 2 * source, count - 1 - 2 * (source - half))
    place = ((source - col * half) % count).astype(jnp.int32)

    slot = (row - col * half) % count
    lane = jnp.arange(keys, dtype=jnp.int32)
    valid = jnp.where(lane // rows == slot, jnp.tile(token_mask, count), 0).astype(BF16)
    valid_width = min(keys, 512)
    valid = valid.reshape(keys // valid_width, valid_width)
    valid = jnp.pad(valid, ((0, 8 - valid.shape[0]), (0, width - valid_width)))

    block = mix(col_index, tokens_in, cond_single, w_scale, w_shift, valid, local)

    near_bias = pair_bias_of(pair_cond, w_pair)
    far_bias = swap(near_bias)
    key_weights = (w_key, swap(w_key), w_value, swap(w_value))

    blocks = [block]
    held = project_kv(place, 0, [block], key_weights, None, local, rows, keys)
    ahead = behind = block
    for k in range(1, half + 1):
        ahead = lax.ppermute(ahead, "row", forward)
        arrived = [ahead]
        if k < half:
            behind = lax.ppermute(behind, "row", backward)
            arrived.append(behind)
        held = project_kv(place, len(blocks), arrived, key_weights, held, local, rows, keys)
        blocks += arrived

    query, gate, out_gate = project_q(
        block, (w_query, swap(w_query), w_gate, swap(w_gate)), cond_single, w_outgate, local * rows
    )

    atoms = atom_cond.shape[0]
    windows = window_start.shape[0]
    chip = 2 * atoms
    first = row * chip
    own_first = first + col * atoms
    atom_index = own_first + jnp.arange(atoms, dtype=jnp.int32)
    window_index = own_first // WQ + jnp.arange(windows, dtype=jnp.int32)
    ints = jnp.stack(
        [
            atom_token - atom_index // PER_TOKEN,
            atom_mask,
            jnp.pad(window_start - window_index * WQ, (0, atoms - windows)),
        ]
    )
    ints = jnp.pad(ints, ((0, 5), (0, 0))).astype(BF16)
    packed = jnp.concatenate([atom_cond, ints], axis=0)
    packed_other = swap(packed)
    lower = jnp.where(col == 0, packed, packed_other)
    upper = jnp.where(col == 0, packed_other, packed)
    chip_cond = jnp.concatenate([lower[:atoms], upper[:atoms]], axis=0)
    chip_ints = jnp.concatenate([lower[atoms:], upper[atoms:]], axis=1)
    top = jnp.pad(chip_ints[:1, :HALO], ((0, 7), (0, atoms - HALO)))
    bottom = jnp.pad(chip_ints[:1, chip - HALO :], ((0, 7), (0, atoms - HALO)))
    top = jnp.concatenate([chip_cond[:HALO], top], axis=0)
    bottom = jnp.concatenate([chip_cond[chip - HALO :], bottom], axis=0)
    up = [(i, i + 1) for i in range(count - 1)]
    down = [(i + 1, i) for i in range(count - 1)]
    before = lax.ppermute(bottom, "row", up)
    after = lax.ppermute(top, "row", down)
    cond_wide = jnp.concatenate([before[:HALO], chip_cond, after[:HALO]], axis=0)
    delta = jnp.concatenate(
        [before[HALO, :HALO], chip_ints[0], after[HALO, :HALO]], axis=0
    ).astype(jnp.int32)
    extent = chip + 2 * HALO
    wide_index = first - HALO + jnp.arange(extent, dtype=jnp.int32)
    token = delta + lax.shift_right_arithmetic(wide_index, 3) - (row - 1) * rows
    pick = (token[:, None] == jnp.arange(3 * rows, dtype=jnp.int32)[None, :]).astype(BF16)
    live = chip_ints[1:2].astype(F32)
    chip_windows = 2 * windows
    order = jnp.arange(chip_windows, dtype=jnp.int32)
    shifts = jnp.concatenate([lower[atoms + 2, :windows], upper[atoms + 2, :windows]], axis=0)
    base = jnp.clip(order * WQ - WQ, 0, extent - SPAN)
    offset = shifts.astype(jnp.int32) + order * WQ + HALO - base
    window = (
        offset[:, None, None] + jnp.arange(WK, dtype=jnp.int32)[None, :, None]
        == jnp.arange(SPAN, dtype=jnp.int32)[None, None, :]
    ).astype(BF16)
    atom_scale, atom_shift = atom_cond_of(cond_wide, w_ascale, w_ashift)
    atom_bias = in_order(atom_bias_of(atom_pair, w_apair), 0)

    tokens, projected = attend(
        col_index, query, *held, near_bias, far_bias, gate, out_gate, tokens_in,
        (w_out, swap(w_out)), w_token_atom, blocks, valid_width,
    )
    left = lax.ppermute(projected, "row", up)
    right = lax.ppermute(projected, "row", down)
    tokens_out = in_order(tokens, 0)
    keep, send = decode(
        col_index, left, projected, right, pick, window, cond_wide, atom_scale, atom_shift, atom_bias,
        live, (w_aquery, w_akey, w_avalue, w_agate, w_aout, w_update),
    )
    theirs = swap(send)
    atom_update = jnp.where(
        col == 0,
        jnp.concatenate([keep, theirs], axis=0),
        jnp.concatenate([theirs, keep], axis=0),
    )
    return (tokens_out, atom_update)


def solution(mesh):
    return jax.shard_map(
        shards,
        mesh=mesh,
        in_specs=(
            P("groups", "row", None),
            P(("groups", "row"), None),
            P(("groups", "row")),
            P(("groups", "row"), "col", None),
            P(),
            P(),
            P(),
            P(),
            P(None, "col"),
            P(None, "col"),
            P(None, "col"),
            P(None, "col"),
            P("col", None),
            P(("groups", "row", "col"), None),
            P(("groups", "row", "col")),
            P(("groups", "row", "col")),
            P(("groups", "row", "col")),
            P(("groups", "row", "col"), None, None, None),
            P(),
            P(),
            P(),
            P(),
            P(),
            P(),
            P(),
            P(),
            P(),
            P(),
        ),
        out_specs=(P("groups", "row", None), P("groups", None, ("row", "col"))),
        check_vma=False,
    )
```
